256 devices in a mesh: frame: 16 (over z, core), row: 16 (over x, y).
Axes of the slice: x: 4, y: 4, z: 8, core: 2. Of those that a mesh axis runs over, the one named last changes fastest.
Arguments:
- queries: bfloat16 [32, 64, 64, 2240], P('frame', 'row'), may hold values from -6 to 6
- keys: bfloat16 [32, 64, 64, 2240], P('frame', 'row'), may hold values from -12 to 12
- values: bfloat16 [32, 64, 64, 2240], P('frame', 'row'), may hold values from -12 to 12
- gate: bfloat16 [32, 64, 64, 2240], P('frame', 'row'), may hold values from -8 to 8
- conv_weight: float32 [3, 3, 2240], replicated, may hold values from -2 to 2
Outputs:
- mixed: bfloat16 [32, 64, 64, 2240], P('frame', 'row')
The draws below stay inside these ranges and needn't reach their ends.
All inputs are finite; a program needn't handle non-finite values.
Results may differ from the reference program's by a relative error of at most 0.005.
Values may be sent and summed in bfloat16 or wider, within the bound.
A program may use at most 128 MiB of HBM per device.

```python
import jax
import jax.numpy as jnp
from jax import lax

HEADS = 70
HEAD_DIM = 32
D = 2240
WIDTH = 64
FRAMES = 32
ROWS = 64


def draw_keys(key, part):
    shape = (FRAMES, ROWS, WIDTH, HEADS * HEAD_DIM)
    rise = 1.0 + 2.0 * jnp.arange(FRAMES, dtype=jnp.float32) / (FRAMES - 1)
    base = jnp.clip(jax.random.normal(jax.random.fold_in(key, 11), shape, jnp.float32), -4.0, 4.0)
    return jnp.clip(base * rise[:, None, None, None], -12.0, 12.0).astype(jnp.bfloat16)


def draw_values(key, part):
    shape = (FRAMES, ROWS, WIDTH, HEADS * HEAD_DIM)
    noise = jax.random.normal(jax.random.fold_in(key, 21), shape, jnp.float32)
    offset = 3.0 * jax.random.normal(jax.random.fold_in(key, 22), (FRAMES, ROWS, 1, HEADS * HEAD_DIM), jnp.float32)
    return jnp.clip(noise + offset, -12.0, 12.0).astype(jnp.bfloat16)


def block_levels(stream_key, shape, cuts, low, largest):
    level = 1.0
    for position, parts in cuts:
        steps = jax.random.uniform(jax.random.fold_in(jax.random.fold_in(stream_key, 6), position), (parts,), jnp.float32, low / len(cuts), largest / len(cuts))
        level = level * jnp.repeat(jnp.exp(steps), shape[position] // parts).reshape((-1,) + (1,) * (len(shape) - 1 - position))
    return level


def gaussian(own_key, extent, width, bound, split=(), kind=jnp.bfloat16):
    array = width * jax.random.normal(own_key, extent, jnp.float32)
    if split:
        array = array * block_levels(own_key, extent, split, -0.22, 0.18)
    return jnp.clip(array, -bound, bound).astype(kind)


def setup_inputs(seed: int = 0) -> dict:
    arg_keys = jax.random.split(jax.random.key(seed), 6)
    queries = gaussian(arg_keys[0], (FRAMES, ROWS, WIDTH, D), 1.0, 6.0, ((0, 16), (1, 16)))
    keys = draw_keys(jax.random.fold_in(arg_keys[5], 71), 0)
    values = draw_values(jax.random.fold_in(arg_keys[5], 71), 0)
    gate = gaussian(arg_keys[3], (FRAMES, ROWS, WIDTH, D), 1.5, 8.0, ((0, 16), (1, 16)))
    conv_weight = gaussian(arg_keys[4], (3, 3, D), 9 ** -0.5, 2.0, (), jnp.float32)
    return {"queries": queries, "keys": keys, "values": values, "gate": gate, "conv_weight": conv_weight}


def frame_sums(pair):
    keyf, valf = pair
    kf = jax.nn.relu(keyf).astype(jnp.float32).reshape(ROWS * WIDTH, HEADS, HEAD_DIM)
    vf = valf.astype(jnp.float32).reshape(ROWS * WIDTH, HEADS, HEAD_DIM)
    partial_value = jnp.einsum("thd,the->hde", kf, vf, precision=lax.Precision.HIGHEST)
    return partial_value, jnp.sum(kf, axis=0)


def frame_out(items):
    query, states, zsum, gatef, conv_weight = items
    qf = jax.nn.relu(query).astype(jnp.float32).reshape(ROWS * WIDTH, HEADS, HEAD_DIM)
    numer = jnp.einsum("thd,hde->the", qf, states, precision=lax.Precision.HIGHEST)
    denom = jnp.einsum("thd,hd->th", qf, zsum, precision=lax.Precision.HIGHEST)
    attended = (numer / (denom[:, :, None] + 1e-6)).reshape(ROWS, WIDTH, HEADS * HEAD_DIM).astype(jnp.bfloat16)
    padded = jnp.pad(attended, ((1, 1), (1, 1), (0, 0))).astype(jnp.float32)
    conv = jnp.zeros((ROWS, WIDTH, HEADS * HEAD_DIM), jnp.float32)
    for a in range(3):
        for b in range(3):
            conv = conv + conv_weight[a, b] * padded[a:a + ROWS, b:b + WIDTH]
    return (conv * jax.nn.silu(gatef.astype(jnp.float32))).astype(jnp.bfloat16)


def reference(queries, keys, values, gate, conv_weight):
    partial_value, norm_part = lax.map(frame_sums, (keys, values))
    states = jnp.cumsum(partial_value, axis=0)
    zsum = jnp.cumsum(norm_part, axis=0)
    weights = jnp.broadcast_to(conv_weight, (queries.shape[0],) + conv_weight.shape)
    return lax.map(frame_out, (queries, states, zsum, gate, weights))
```

```python
import jax
import jax.numpy as jnp
from jax import lax
from jax.experimental import pallas as pl
from jax.experimental.pallas import tpu as pltpu
from jax.sharding import PartitionSpec as P

HEADS = 70
HEAD_DIM = 32
MESH = pl.DeviceIdType.MESH

GROUP = 256
PACKED = 2560
NORM_AT = 2304
CHUNK = 640
SIDE = 4


def sums_kernel(
    n_frame, n_row, q_ref, k_ref, v_ref, halo_ref, states_ref,
    k_buf, v_buf, part, rx, total, pair_rx, chip_total, chip_rx, before, mine,
    load_sem, halo_send, halo_recv, rs_send, rs_recv, pair_send, pair_recv,
    chip_send, chip_recv, ag_send, ag_recv, own_sem,
):
    frame = lax.axis_index("frame")
    row = lax.axis_index("row")
    core = lax.rem(frame, 2)
    chip = frame // 2
    n_chip = n_frame // 2
    partner = frame + 1 - 2 * core
    channels = k_buf.shape[-1]

    loads = []
    for f in range(2):
        loads.append(pltpu.make_async_copy(k_ref.at[f], k_buf.at[f], load_sem.at[0, f]))
        loads.append(pltpu.make_async_copy(v_ref.at[f], v_buf.at[f], load_sem.at[1, f]))
    for load in loads:
        load.start()

    barrier = pltpu.get_barrier_semaphore()

    @pl.loop(1, n_row)
    def _(i):
        pl.semaphore_signal(
            barrier, inc=1, device_id=(frame, lax.rem(row + i, n_row)), device_id_type=MESH
        )

    @pl.loop(1, n_chip)
    def _(i):
        pl.semaphore_signal(
            barrier, inc=1, device_id=(lax.rem(frame + 2 * i, n_frame), row), device_id_type=MESH
        )

    pl.semaphore_signal(barrier, inc=1, device_id=(partner, row), device_id_type=MESH)

    def halo(side, f):
        source, target = (3, row + 1) if side == 0 else (0, row - 1)
        return pltpu.make_async_remote_copy(
            src_ref=q_ref.at[f, source],
            dst_ref=halo_ref.at[side, f],
            send_sem=halo_send.at[side, f],
            recv_sem=halo_recv.at[side, f],
            device_id=(frame, target),
            device_id_type=MESH,
        )

    def halo_start(f):
        @pl.when(row < n_row - 1)
        def _():
            halo(0, f).start()

        @pl.when(row > 0)
        def _():
            halo(1, f).start()

    part[:, channels:] = jnp.zeros((64, PACKED - channels), part.dtype)

    def group(first, width, norms):
        ones = jnp.ones((k_buf.shape[1], 128), jnp.bfloat16)
        heads = width // HEAD_DIM
        lane = lax.broadcasted_iota(jnp.int32, (HEAD_DIM, width), 1) // HEAD_DIM
        slot = lax.broadcasted_iota(jnp.int32, (HEAD_DIM, 128), 1)
        first_head = first // HEAD_DIM
        compact = []
        new_norms = []
        for f in range(2):
            kf = jnp.maximum(k_buf[f, :, pl.ds(first, width)], 0)
            vf = jnp.concatenate([v_buf[f, :, pl.ds(first, width)], ones], axis=1)
            full = lax.dot_general(
                kf, vf, (((0,), (0,)), ((), ())), preferred_element_type=jnp.float32
            )
            state = jnp.zeros((HEAD_DIM, width), jnp.float32)
            norm = norms[f]
            for h in range(heads):
                rows = full[h * HEAD_DIM : (h + 1) * HEAD_DIM]
                state = jnp.where(lane == h, rows[:, :width], state)
                norm = jnp.where(slot == first_head + h, rows[:, width:], norm)
            compact.append(state)
            new_norms.append(norm)
        part[:, pl.ds(first, width)] = interleave(compact).astype(part.dtype)
        return tuple(new_norms)

    def interleave(pair):
        return jnp.concatenate(
            [pair[f][8 * q : 8 * q + 8] for q in range(SIDE) for f in range(2)], axis=0
        )

    for load in loads:
        load.wait()

    whole = channels // GROUP
    early = 3
    norms = tuple(jnp.zeros((HEAD_DIM, 128), jnp.float32) for _ in range(2))

    def step(g, norms):
        return group(pl.multiple_of(g * GROUP, GROUP), GROUP, norms)

    norms = lax.fori_loop(0, early, step, norms)
    pl.semaphore_wait(barrier, n_row - 1 + n_chip)
    halo_start(0)
    norms = lax.fori_loop(early, whole, step, norms)
    norms = group(whole * GROUP, channels - whole * GROUP, norms)
    part[:, NORM_AT : NORM_AT + 128] = interleave(norms).astype(part.dtype)

    def chunk(o):
        return (
            pl.ds(pl.multiple_of(16 * (o // SIDE), 16), 16),
            pl.ds(pl.multiple_of(CHUNK * lax.rem(o, SIDE), 128), CHUNK),
        )

    def scatter(i):
        peer = lax.rem(row + i, n_row)
        return pltpu.make_async_remote_copy(
            src_ref=part.at[chunk(peer)],
            dst_ref=rx.at[i],
            send_sem=rs_send.at[i],
            recv_sem=rs_recv.at[i],
            device_id=(frame, peer),
            device_id_type=MESH,
        )

    @pl.loop(1, n_row)
    def _(i):
        scatter(i).start()

    halo_start(1)

    sums = part[chunk(row)].astype(jnp.float32)

    def add(i, sums):
        scatter(i).wait_recv()
        return sums + rx[i].astype(jnp.float32)

    sums = lax.fori_loop(1, n_row, add, sums)
    even, odd = sums[:8], sums[8:]
    own_total = even + odd
    total[...] = own_total
    pair = pltpu.make_async_remote_copy(
        src_ref=total,
        dst_ref=pair_rx,
        send_sem=pair_send,
        recv_sem=pair_recv,
        device_id=(partner, row),
        device_id_type=MESH,
    )
    pair.start()
    pair.wait_recv()
    other = pair_rx[...]
    chip_total[...] = (own_total + other).astype(chip_total.dtype)

    def pass_on(i):
        return pltpu.make_async_remote_copy(
            src_ref=chip_total,
            dst_ref=chip_rx.at[i],
            send_sem=chip_send.at[i],
            recv_sem=chip_recv.at[i],
            device_id=(frame + 2 * i, row),
            device_id_type=MESH,
        )

    for i in range(1, n_chip):
        @pl.when(chip + i < n_chip)
        def _():
            pass_on(i).start()

    before[...] = jnp.where(core == 1, other, jnp.zeros_like(other))
    for i in range(1, n_chip):
        @pl.when(chip >= i)
        def _():
            pass_on(i).wait_recv()
            before[...] += chip_rx[i].astype(jnp.float32)

    first = before[...] + even
    mine[...] = jnp.concatenate([first, first + odd], axis=0).astype(mine.dtype)
    own = pltpu.make_async_copy(mine, states_ref.at[chunk(row)], own_sem)
    own.start()

    def gather(i):
        return pltpu.make_async_remote_copy(
            src_ref=mine,
            dst_ref=states_ref.at[chunk(row)],
            send_sem=ag_send.at[i],
            recv_sem=ag_recv.at[i],
            device_id=(frame, lax.rem(row + i, n_row)),
            device_id_type=MESH,
        )

    @pl.loop(1, n_row)
    def _(i):
        gather(i).start()

    @pl.loop(1, n_row)
    def _(i):
        gather(i).wait_recv()

    own.wait()

    @pl.when(row > 0)
    def _():
        for f in range(2):
            halo(0, f).wait_recv()
            halo(1, f).wait_send()

    @pl.when(row < n_row - 1)
    def _():
        for f in range(2):
            halo(1, f).wait_recv()
            halo(0, f).wait_send()

    pair.wait_send()
    for i in range(1, n_chip):
        @pl.when(chip + i < n_chip)
        def _():
            pass_on(i).wait_send()

    @pl.loop(1, n_row)
    def _(i):
        scatter(i).wait_send()
        gather(i).wait_send()


def mix_kernel(
    n_row, channels, q_ref, halo_ref, states_ref, norms_ref, gate_ref, weight_ref, out_ref, att
):
    row = lax.axis_index("row")
    g = pl.program_id(0)
    frames, rows, width, lanes = q_ref.shape
    inside = lax.broadcasted_iota(jnp.int32, (1, lanes), 1) < channels - g * lanes
    spread = (
        lax.broadcasted_iota(jnp.int32, (128, lanes), 0)
        == lax.broadcasted_iota(jnp.int32, (128, lanes), 1) // HEAD_DIM + g * (lanes // HEAD_DIM)
    ).astype(jnp.bfloat16)
    same = (
        lax.broadcasted_iota(jnp.int32, (lanes, lanes), 0) // HEAD_DIM
        == lax.broadcasted_iota(jnp.int32, (lanes, lanes), 1) // HEAD_DIM
    )
    states = states_ref[...].astype(jnp.float32)
    norms = jnp.dot(norms_ref[...], spread, preferred_element_type=jnp.float32)

    def blocks(packed, f):
        mine = jnp.concatenate(
            [packed[16 * q + 8 * f : 16 * q + 8 * f + 8] for q in range(SIDE)], axis=0
        )
        tiled = jnp.tile(mine, (lanes // HEAD_DIM, 1))
        return jnp.where(same, tiled, 0.0).astype(jnp.bfloat16)

    def attend(q, state, norm):
        qf = jnp.where(inside, jnp.maximum(q, 0), 0)
        numer = jnp.dot(qf, state, preferred_element_type=jnp.float32)
        denom = jnp.dot(qf, norm, preferred_element_type=jnp.float32)
        return (numer / (denom + 1e-6)).astype(jnp.bfloat16)

    column = lax.broadcasted_iota(jnp.int32, (width, lanes), 0)
    for f in range(frames):
        state, norm = blocks(states, f), blocks(norms, f)
        for r in range(rows):
            att[r + 1] = attend(q_ref[f, r], state, norm)
        top = attend(halo_ref[0, f], state, norm)
        att[0] = jnp.where(row > 0, top, jnp.zeros_like(top))
        bottom = attend(halo_ref[1, f], state, norm)
        att[rows + 1] = jnp.where(row < n_row - 1, bottom, jnp.zeros_like(bottom))
        for r in range(rows):
            three = [att[r + a].astype(jnp.float32) for a in range(3)]
            mixes = []
            for b in range(3):
                total = three[0] * weight_ref[0, b : b + 1]
                for a in range(1, 3):
                    total = total + three[a] * weight_ref[a, b : b + 1]
                mixes.append(total)
            left = jnp.where(column > 0, pltpu.roll(mixes[0], 1, 0), 0.0)
            right = jnp.where(column < width - 1, pltpu.roll(mixes[2], width - 1, 0), 0.0)
            conv = mixes[1] + left + right
            gate = gate_ref[f, r].astype(jnp.float32)
            out_ref[f, r] = (conv * (gate / (1.0 + jnp.exp(-gate)))).astype(out_ref.dtype)


def per_device(n_frame, n_row, queries, keys, values, gate, conv_weight):
    frames, rows, width, channels = queries.shape
    tokens = rows * width
    n_chip = n_frame // 2
    hbm = pl.BlockSpec(memory_space=pl.ANY)
    dma = pltpu.SemaphoreType.DMA
    halo, states = pl.pallas_call(
        lambda *refs: sums_kernel(n_frame, n_row, *refs),
        name="sums",
        out_shape=(
            jax.ShapeDtypeStruct((2, frames, width, channels), jnp.bfloat16),
            jax.ShapeDtypeStruct((64, PACKED), jnp.bfloat16),
        ),
        in_specs=[hbm] * 3,
        out_specs=(hbm, hbm),
        scratch_shapes=[
            pltpu.VMEM((frames, tokens, channels), jnp.bfloat16),
            pltpu.VMEM((frames, tokens, channels), jnp.bfloat16),
            pltpu.VMEM((64, PACKED), jnp.bfloat16),
            pltpu.VMEM((n_row, 16, CHUNK), jnp.bfloat16),
            pltpu.VMEM((8, CHUNK), jnp.float32),
            pltpu.VMEM((8, CHUNK), jnp.float32),
            pltpu.VMEM((8, CHUNK), jnp.bfloat16),
            pltpu.VMEM((n_chip, 8, CHUNK), jnp.bfloat16),
            pltpu.VMEM((8, CHUNK), jnp.float32),
            pltpu.VMEM((16, CHUNK), jnp.bfloat16),
            dma((2, 2)),
            dma((2, 2)),
            dma((2, 2)),
            dma((n_row,)),
            dma((n_row,)),
            dma,
            dma,
            dma((n_chip,)),
            dma((n_chip,)),
            dma((n_row,)),
            dma((n_row,)),
            dma,
        ],
        compiler_params=pltpu.CompilerParams(collective_id=0, has_side_effects=True),
    )(
        queries,
        keys.reshape(frames, tokens, channels),
        values.reshape(frames, tokens, channels),
    )
    lanes = GROUP
    return pl.pallas_call(
        lambda *refs: mix_kernel(n_row, channels, *refs),
        name="mix",
        grid=(pl.cdiv(channels, lanes),),
        out_shape=jax.ShapeDtypeStruct(queries.shape, jnp.bfloat16),
        in_specs=[
            pl.BlockSpec((frames, rows, width, lanes), lambda g: (0, 0, 0, g)),
            pl.BlockSpec((2, frames, width, lanes), lambda g: (0, 0, 0, g)),
            pl.BlockSpec((64, lanes), lambda g: (0, g)),
            pl.BlockSpec((64, 128), lambda g: (0, NORM_AT // 128)),
            pl.BlockSpec((frames, rows, width, lanes), lambda g: (0, 0, 0, g)),
            pl.BlockSpec((3, 3, lanes), lambda g: (0, 0, g)),
        ],
        out_specs=pl.BlockSpec((frames, rows, width, lanes), lambda g: (0, 0, 0, g)),
        scratch_shapes=[pltpu.VMEM((rows + 2, width, lanes), jnp.bfloat16)],
    )(queries, halo, states, states, gate, conv_weight)


def solution(mesh):
    split = P("frame", "row", None, None)
    sizes = (mesh.shape["frame"], mesh.shape["row"])
    return jax.shard_map(
        lambda *arrays: per_device(*sizes, *arrays),
        mesh=mesh,
        in_specs=(split, split, split, split, P()),
        out_specs=split,
        check_vma=False,
    )
```

```python
import jax
import jax.numpy as jnp
from jax import lax
from jax.experimental import pallas as pl
from jax.experimental.pallas import tpu as pltpu
from jax.sharding import PartitionSpec as P

HEADS = 70
HEAD_DIM = 32
MESH = pl.DeviceIdType.MESH

GROUP = 256
PACKED = 2560
NORM_AT = 2304
CHUNK = 640
HALO_EARLY = 0
SIDE = 4


def mixer_kernel(
    n_frame, n_row, q_ref, k_ref, v_ref, gate_ref, weight_ref, out_ref,
    k_buf, v_buf, gate_buf, q_buf, silu_buf, weight_buf, halo_buf, att, states_buf, part, rx, total, pair_rx, chip_total, chip_rx, before, mine,
    load_sem, halo_send, halo_recv, rs_send, rs_recv, pair_send, pair_recv,
    chip_send, chip_recv, ag_send, ag_recv, own_sem, gate_sem, q_sem,
    weight_sem,
):
    frame = lax.axis_index("frame")
    row = lax.axis_index("row")
    core = lax.rem(frame, 2)
    chip = frame // 2
    n_chip = n_frame // 2
    partner = frame + 1 - 2 * core
    channels = k_buf.shape[-1]

    barrier = pltpu.get_barrier_semaphore()

    @pl.loop(1, n_row)
    def _(i):
        pl.semaphore_signal(
            barrier, inc=1, device_id=(frame, lax.rem(row + i, n_row)), device_id_type=MESH
        )

    @pl.loop(1, n_chip)
    def _(i):
        pl.semaphore_signal(
            barrier, inc=1, device_id=(lax.rem(frame + 2 * i, n_frame), row), device_id_type=MESH
        )

    pl.semaphore_signal(barrier, inc=1, device_id=(partner, row), device_id_type=MESH)

    stages = (0, 768, 1536, channels)
    loads = []
    for at, (low, high) in enumerate(zip(stages, stages[1:])):
        lanes = pl.ds(low, high - low)
        loads.append(
            [
                pltpu.make_async_copy(src.at[:, :, lanes], dst.at[:, :, lanes], load_sem.at[at, i])
                for i, (src, dst) in enumerate(((k_ref, k_buf), (v_ref, v_buf)))
            ]
        )
        for load in loads[-1]:
            load.start()
    gate_load = pltpu.make_async_copy(gate_ref, gate_buf, gate_sem)
    gate_load.start()
    q_load = pltpu.make_async_copy(q_ref, q_buf, q_sem)
    q_load.start()
    weight_load = pltpu.make_async_copy(weight_ref, weight_buf, weight_sem)
    weight_load.start()

    whole = channels // GROUP
    tail = channels - whole * GROUP

    def halo(side, g, lanes):
        source, target = (3, row + 1) if side == 0 else (0, row - 1)
        first = g * GROUP if lanes < GROUP else pl.multiple_of(g * GROUP, GROUP)
        cut = pl.ds(first, lanes)
        return pltpu.make_async_remote_copy(
            src_ref=q_buf.at[:, source, :, cut],
            dst_ref=halo_buf.at[side, :, :, cut],
            send_sem=halo_send.at[side, g],
            recv_sem=halo_recv.at[side, g],
            device_id=(frame, target),
            device_id_type=MESH,
        )

    def halo_start(low, high):
        def both(g, lanes):
            @pl.when(row < n_row - 1)
            def _():
                halo(0, g, lanes).start()

            @pl.when(row > 0)
            def _():
                halo(1, g, lanes).start()

        @pl.loop(low, min(high, whole))
        def _(g):
            both(g, GROUP)

        if high > whole:
            both(whole, tail)

    part[:, channels:] = jnp.zeros((64, PACKED - channels), part.dtype)

    def group(first, width, norms):
        ones = jnp.ones((k_buf.shape[1], 128), jnp.bfloat16)
        heads = width // HEAD_DIM
        lane = lax.broadcasted_iota(jnp.int32, (HEAD_DIM, width), 1) // HEAD_DIM
        slot = lax.broadcasted_iota(jnp.int32, (HEAD_DIM, 128), 1)
        first_head = first // HEAD_DIM
        compact = []
        new_norms = []
        for f in range(2):
            kf = jnp.maximum(k_buf[f, :, pl.ds(first, width)], 0)
            vf = jnp.concatenate([v_buf[f, :, pl.ds(first, width)], ones], axis=1)
            full = lax.dot_general(
                kf, vf, (((0,), (0,)), ((), ())), preferred_element_type=jnp.float32
            )
            state = jnp.zeros((HEAD_DIM, width), jnp.float32)
            norm = norms[f]
            for h in range(heads):
                rows = full[h * HEAD_DIM : (h + 1) * HEAD_DIM]
                state = jnp.where(lane == h, rows[:, :width], state)
                norm = jnp.where(slot == first_head + h, rows[:, width:], norm)
            compact.append(state)
            new_norms.append(norm)
        part[:, pl.ds(first, width)] = interleave(compact).astype(part.dtype)
        return tuple(new_norms)

    def interleave(pair):
        return jnp.concatenate(
            [pair[f][8 * q : 8 * q + 8] for q in range(SIDE) for f in range(2)], axis=0
        )

    def chunk(o):
        return (
            pl.ds(pl.multiple_of(16 * (o // SIDE), 16), 16),
            pl.ds(pl.multiple_of(CHUNK * lax.rem(o, SIDE), 128), CHUNK),
        )

    def scatter(peer):
        i = lax.rem(peer - row + n_row, n_row)
        return pltpu.make_async_remote_copy(
            src_ref=part.at[chunk(peer)],
            dst_ref=rx.at[i],
            send_sem=rs_send.at[i],
            recv_sem=rs_recv.at[i],
            device_id=(frame, peer),
            device_id_type=MESH,
        )

    def scatter_start(j):
        for i in range(SIDE):
            peer = lax.rem(row // SIDE + i + 1, SIDE) * SIDE + j
            if i < SIDE - 1:
                scatter(peer).start()
            else:
                @pl.when(peer != row)
                def _():
                    scatter(peer).start()

    norms = tuple(jnp.zeros((HEAD_DIM, 128), jnp.float32) for _ in range(2))

    def step(g, norms):
        return group(pl.multiple_of(g * GROUP, GROUP), GROUP, norms)

    for load in loads[0]:
        load.wait()
    norms = lax.fori_loop(0, 3, step, norms)
    for load in loads[1]:
        load.wait()
    norms = lax.fori_loop(3, 5, step, norms)
    pl.semaphore_wait(barrier, n_row - 1 + n_chip)
    scatter_start(0)
    scatter_start(1)
    for load in loads[2]:
        load.wait()
    norms = lax.fori_loop(5, 8, step, norms)
    scatter_start(2)
    norms = group(8 * GROUP, channels - 8 * GROUP, norms)
    part[:, NORM_AT : NORM_AT + 128] = interleave(norms).astype(part.dtype)
    scatter_start(3)

    @pl.when(row == 0)
    def _():
        halo_buf[0] = jnp.zeros_like(halo_buf[0])

    @pl.when(row == n_row - 1)
    def _():
        halo_buf[1] = jnp.zeros_like(halo_buf[1])

    gate_load.wait()
    frames, rows, width = q_buf.shape[:3]
    for f in range(frames):
        for r in range(rows):
            @pl.loop(0, width // 16)
            def _(i):
                cut = pl.ds(pl.multiple_of(16 * i, 16), 16)
                gate = gate_buf[f, r, cut].astype(jnp.float32)
                silu_buf[f, r, cut] = gate / (1.0 + jnp.exp(-gate))

    sums = part[chunk(row)].astype(jnp.float32)

    def add(i, sums):
        scatter(lax.rem(row + i, n_row)).wait_recv()
        return sums + rx[i].astype(jnp.float32)

    sums = lax.fori_loop(1, n_row, add, sums)
    q_load.wait()
    halo_start(0, HALO_EARLY)
    even, odd = sums[:8], sums[8:]
    own_total = even + odd
    total[...] = own_total
    pair = pltpu.make_async_remote_copy(
        src_ref=total,
        dst_ref=pair_rx,
        send_sem=pair_send,
        recv_sem=pair_recv,
        device_id=(partner, row),
        device_id_type=MESH,
    )
    pair.start()
    pair.wait_recv()
    other = pair_rx[...]
    chip_total[...] = (own_total + other).astype(chip_total.dtype)

    def pass_on(i):
        return pltpu.make_async_remote_copy(
            src_ref=chip_total,
            dst_ref=chip_rx.at[i],
            send_sem=chip_send.at[i],
            recv_sem=chip_recv.at[i],
            device_id=(frame + 2 * i, row),
            device_id_type=MESH,
        )

    for i in range(1, n_chip):
        @pl.when(chip + i < n_chip)
        def _():
            pass_on(i).start()

    before[...] = jnp.where(core == 1, other, jnp.zeros_like(other))
    for i in range(1, n_chip):
        @pl.when(chip >= i)
        def _():
            pass_on(i).wait_recv()
            before[...] += chip_rx[i].astype(jnp.float32)

    first = before[...] + even
    mine[...] = jnp.concatenate([first, first + odd], axis=0).astype(mine.dtype)
    own = pltpu.make_async_copy(mine, states_buf.at[chunk(row)], own_sem)
    own.start()

    def gather(i):
        return pltpu.make_async_remote_copy(
            src_ref=mine,
            dst_ref=states_buf.at[chunk(row)],
            send_sem=ag_send.at[i],
            recv_sem=ag_recv.at[i],
            device_id=(frame, lax.rem(row + i, n_row)),
            device_id_type=MESH,
        )

    @pl.loop(1, n_row)
    def _(i):
        gather(i).start()

    halo_start(HALO_EARLY, whole + 1)

    @pl.loop(1, n_row)
    def _(i):
        gather(i).wait_recv()

    own.wait()
    weight_load.wait()
    half = 128
    edge = lax.broadcasted_iota(jnp.int32, (8, half), 0)

    def attend(first, lanes, sources):
        heads = lanes // HEAD_DIM
        cut = pl.ds(first, lanes)
        spread = (
            lax.broadcasted_iota(jnp.int32, (128, lanes), 0)
            == lax.broadcasted_iota(jnp.int32, (128, lanes), 1) // HEAD_DIM + first // HEAD_DIM
        ).astype(jnp.bfloat16)
        same = (
            lax.broadcasted_iota(jnp.int32, (lanes, lanes), 0) // HEAD_DIM
            == lax.broadcasted_iota(jnp.int32, (lanes, lanes), 1) // HEAD_DIM
        )
        states = states_buf[:, cut].astype(jnp.float32)
        norms = jnp.dot(
            states_buf[:, NORM_AT : NORM_AT + 128], spread, preferred_element_type=jnp.float32
        )

        def blocks(packed, f):
            mine = jnp.concatenate(
                [packed[16 * q + 8 * f : 16 * q + 8 * f + 8] for q in range(SIDE)], axis=0
            )
            return jnp.where(same, jnp.tile(mine, (heads, 1)), 0.0).astype(jnp.bfloat16)

        for f in range(frames):
            state, norm = blocks(states, f), blocks(norms, f)
            for r, source in sources(f):
                qf = jnp.maximum(source[:, cut], 0)
                numer = jnp.dot(qf, state, preferred_element_type=jnp.float32)
                denom = jnp.dot(qf, norm, preferred_element_type=jnp.float32)
                att[f, r, :, cut] = numer / (denom + 1e-6)

    def mix(first, lanes, which):
        for low in range(0, lanes, half):
            wide = min(half, lanes - low)
            cut = pl.ds(first + low, wide)
            weights = [[weight_buf[a, b : b + 1, cut] for b in range(3)] for a in range(3)]
            for f in range(frames):
                for r in which:
                    three = [att[f, r + a, :, cut] for a in range(3)]
                    mixes = []
                    for b in range(3):
                        total = three[0] * weights[0][b]
                        for a in range(1, 3):
                            total = total + three[a] * weights[a][b]
                        mixes.append(total)
                    left = pltpu.roll(mixes[0], 1, 0)
                    first_rows = jnp.where(edge[:, :wide] > 0, left[:8], 0.0)
                    left = jnp.concatenate([first_rows, left[8:]], axis=0)
                    right = pltpu.roll(mixes[2], width - 1, 0)
                    last_rows = jnp.where(edge[:, :wide] < 7, right[-8:], 0.0)
                    right = jnp.concatenate([right[:-8], last_rows], axis=0)
                    conv = mixes[1] + left + right
                    out_ref[f, r, :, cut] = (conv * silu_buf[f, r, :, cut]).astype(out_ref.dtype)

    def inner(first, lanes):
        attend(first, lanes, lambda f: [(r + 1, q_buf.at[f, r]) for r in range(rows)])
        mix(first, lanes, range(1, rows - 1))

    def outer(g, first, lanes):
        @pl.when(row > 0)
        def _():
            halo(0, g, lanes).wait_recv()

        @pl.when(row < n_row - 1)
        def _():
            halo(1, g, lanes).wait_recv()

        attend(first, lanes, lambda f: [(0, halo_buf.at[0, f]), (rows + 1, halo_buf.at[1, f])])
        mix(first, lanes, (0, rows - 1))

    @pl.loop(0, whole)
    def _(g):
        inner(pl.multiple_of(g * GROUP, GROUP), GROUP)

    inner(whole * GROUP, tail)

    @pl.loop(0, whole)
    def _(g):
        outer(g, pl.multiple_of(g * GROUP, GROUP), GROUP)

    outer(whole, whole * GROUP, tail)

    @pl.loop(0, whole)
    def _(g):
        @pl.when(row < n_row - 1)
        def _():
            halo(0, g, GROUP).wait_send()

        @pl.when(row > 0)
        def _():
            halo(1, g, GROUP).wait_send()

    @pl.when(row < n_row - 1)
    def _():
        halo(0, whole, tail).wait_send()

    @pl.when(row > 0)
    def _():
        halo(1, whole, tail).wait_send()

    pair.wait_send()
    for i in range(1, n_chip):
        @pl.when(chip + i < n_chip)
        def _():
            pass_on(i).wait_send()

    @pl.loop(1, n_row)
    def _(i):
        scatter(lax.rem(row + i, n_row)).wait_send()
        gather(i).wait_send()


def per_device(n_frame, n_row, queries, keys, values, gate, conv_weight):
    frames, rows, width, channels = queries.shape
    tokens = rows * width
    n_chip = n_frame // 2
    groups = pl.cdiv(channels, GROUP)
    dma = pltpu.SemaphoreType.DMA
    flat = (frames, tokens, channels)
    arrays = (queries, keys.reshape(flat), values.reshape(flat), gate, conv_weight)
    return pl.pallas_call(
        lambda *refs: mixer_kernel(n_frame, n_row, *refs),
        name="mixer",
        out_shape=pltpu.VMEM(queries.shape, jnp.bfloat16),
        in_specs=[pl.BlockSpec(memory_space=pltpu.HBM)] * len(arrays),
        out_specs=pl.BlockSpec(memory_space=pltpu.VMEM),
        scratch_shapes=[
            pltpu.VMEM(flat, jnp.bfloat16),
            pltpu.VMEM(flat, jnp.bfloat16),
            pltpu.VMEM(gate.shape, jnp.bfloat16),
            pltpu.VMEM(queries.shape, jnp.bfloat16),
            pltpu.VMEM(queries.shape, jnp.float32),
            pltpu.VMEM(conv_weight.shape, jnp.float32),
            pltpu.VMEM((2, frames, width, channels), jnp.bfloat16),
            pltpu.VMEM((frames, rows + 2, width, channels), jnp.float32),
            pltpu.VMEM((64, PACKED), jnp.bfloat16),
            pltpu.VMEM((64, PACKED), jnp.bfloat16),
            pltpu.VMEM((n_row, 16, CHUNK), jnp.bfloat16),
            pltpu.VMEM((8, CHUNK), jnp.float32),
            pltpu.VMEM((8, CHUNK), jnp.float32),
            pltpu.VMEM((8, CHUNK), jnp.bfloat16),
            pltpu.VMEM((n_chip, 8, CHUNK), jnp.bfloat16),
            pltpu.VMEM((8, CHUNK), jnp.float32),
            pltpu.VMEM((16, CHUNK), jnp.bfloat16),
            dma((3, 2)),
            dma((2, groups)),
            dma((2, groups)),
            dma((n_row,)),
            dma((n_row,)),
            dma,
            dma,
            dma((n_chip,)),
            dma((n_chip,)),
            dma((n_row,)),
            dma((n_row,)),
            dma,
            dma,
            dma,
            dma,
        ],
        compiler_params=pltpu.CompilerParams(
            collective_id=0, has_side_effects=True, vmem_limit_bytes=40 << 20
        ),
    )(*(pltpu.with_memory_space_constraint(a, pltpu.HBM) for a in arrays))


def solution(mesh):
    split = P("frame", "row", None, None)
    sizes = (mesh.shape["frame"], mesh.shape["row"])
    return jax.shard_map(
        lambda *arrays: per_device(*sizes, *arrays),
        mesh=mesh,
        in_specs=(split, split, split, split, P()),
        out_specs=split,
        check_vma=False,
    )
```

```python
import jax
import jax.numpy as jnp
from jax import lax
from jax.experimental import pallas as pl
from jax.experimental.pallas import tpu as pltpu
from jax.sharding import PartitionSpec as P

HEADS = 70
HEAD_DIM = 32
MESH = pl.DeviceIdType.MESH

GROUP = 256
PACKED = 2560
NORM_AT = 2304
CHUNK = 640
HALO_EARLY = 1
HALO_MORE = 2
SIDE = 4


def mixer_kernel(
    n_frame, n_row, q_ref, k_ref, v_ref, gate_ref, weight_ref, out_ref,
    k_buf, v_buf, gate_buf, q_buf, silu_buf, weight_buf, halo_buf, att_00, att_01, att_10, att_11, states_buf, part, rx, total, pair_rx, chip_total, chip_rx, before, mine,
    load_sem, halo_send, halo_recv, rs_send, rs_recv, pair_send, pair_recv,
    chip_send, chip_recv, ag_send, ag_recv, own_sem, gate_sem, q_sem,
    weight_sem,
):
    frame = lax.axis_index("frame")
    row = lax.axis_index("row")
    core = lax.rem(frame, 2)
    chip = frame // 2
    n_chip = n_frame // 2
    partner = frame + 1 - 2 * core
    channels = k_buf.shape[-1]

    barrier = pltpu.get_barrier_semaphore()

    @pl.loop(1, n_row)
    def _(i):
        pl.semaphore_signal(
            barrier, inc=1, device_id=(frame, lax.rem(row + i, n_row)), device_id_type=MESH
        )

    @pl.loop(1, n_chip)
    def _(i):
        pl.semaphore_signal(
            barrier, inc=1, device_id=(lax.rem(frame + 2 * i, n_frame), row), device_id_type=MESH
        )

    pl.semaphore_signal(barrier, inc=1, device_id=(partner, row), device_id_type=MESH)

    stages = (0, 768, 1536, channels)
    q_load = pltpu.make_async_copy(q_ref, q_buf, q_sem)
    loads = []
    for at, (low, high) in enumerate(zip(stages, stages[1:])):
        lanes = pl.ds(low, high - low)
        loads.append(
            [
                pltpu.make_async_copy(src.at[:, :, lanes], dst.at[:, :, lanes], load_sem.at[at, i])
                for i, (src, dst) in enumerate(((k_ref, k_buf), (v_ref, v_buf)))
            ]
        )
        for load in loads[-1]:
            load.start()
        if at == 1:
            q_load.start()
    gate_load = pltpu.make_async_copy(gate_ref, gate_buf, gate_sem)
    gate_load.start()
    weight_load = pltpu.make_async_copy(weight_ref, weight_buf, weight_sem)
    weight_load.start()

    whole = channels // GROUP
    tail = channels - whole * GROUP

    def halo(side, g, lanes):
        source, target = (3, row + 1) if side == 0 else (0, row - 1)
        first = g * GROUP if lanes < GROUP else pl.multiple_of(g * GROUP, GROUP)
        cut = pl.ds(first, lanes)
        return pltpu.make_async_remote_copy(
            src_ref=q_buf.at[:, source, :, cut],
            dst_ref=halo_buf.at[side, :, :, cut],
            send_sem=halo_send.at[side, g],
            recv_sem=halo_recv.at[side, g],
            device_id=(frame, target),
            device_id_type=MESH,
        )

    def halo_start(low, high):
        def both(g, lanes):
            @pl.when(row < n_row - 1)
            def _():
                halo(0, g, lanes).start()

            @pl.when(row > 0)
            def _():
                halo(1, g, lanes).start()

        @pl.loop(low, min(high, whole))
        def _(g):
            both(g, GROUP)

        if high > whole:
            both(whole, tail)

    part[:, channels:] = jnp.zeros((64, PACKED - channels), part.dtype)

    def group(first, width, norms):
        ones = jnp.ones((k_buf.shape[1], 128), jnp.bfloat16)
        heads = width // HEAD_DIM
        lane = lax.broadcasted_iota(jnp.int32, (HEAD_DIM, width), 1) // HEAD_DIM
        slot = lax.broadcasted_iota(jnp.int32, (HEAD_DIM, 128), 1)
        first_head = first // HEAD_DIM
        compact = []
        new_norms = []
        for f in range(2):
            kf = jnp.maximum(k_buf[f, :, pl.ds(first, width)], 0)
            vf = jnp.concatenate([v_buf[f, :, pl.ds(first, width)], ones], axis=1)
            full = lax.dot_general(
                kf, vf, (((0,), (0,)), ((), ())), preferred_element_type=jnp.float32
            )
            state = jnp.zeros((HEAD_DIM, width), jnp.float32)
            norm = norms[f]
            for h in range(heads):
                rows = full[h * HEAD_DIM : (h + 1) * HEAD_DIM]
                state = jnp.where(lane == h, rows[:, :width], state)
                norm = jnp.where(slot == first_head + h, rows[:, width:], norm)
            compact.append(state)
            new_norms.append(norm)
        part[:, pl.ds(first, width)] = interleave(compact).astype(part.dtype)
        return tuple(new_norms)

    def interleave(pair):
        return jnp.concatenate(
            [pair[f][8 * q : 8 * q + 8] for q in range(SIDE) for f in range(2)], axis=0
        )

    def chunk(o):
        return (
            pl.ds(pl.multiple_of(16 * (o // SIDE), 16), 16),
            pl.ds(pl.multiple_of(CHUNK * lax.rem(o, SIDE), 128), CHUNK),
        )

    def scatter(peer):
        i = lax.rem(peer - row + n_row, n_row)
        return pltpu.make_async_remote_copy(
            src_ref=part.at[chunk(peer)],
            dst_ref=rx.at[i],
            send_sem=rs_send.at[i],
            recv_sem=rs_recv.at[i],
            device_id=(frame, peer),
            device_id_type=MESH,
        )

    def scatter_start(j):
        for i in range(SIDE):
            peer = lax.rem(row // SIDE + i + 1, SIDE) * SIDE + j
            if i < SIDE - 1:
                scatter(peer).start()
            else:
                @pl.when(peer != row)
                def _():
                    scatter(peer).start()

    norms = tuple(jnp.zeros((HEAD_DIM, 128), jnp.float32) for _ in range(2))

    def step(g, norms):
        return group(pl.multiple_of(g * GROUP, GROUP), GROUP, norms)

    for load in loads[0]:
        load.wait()
    norms = lax.fori_loop(0, 3, step, norms)
    for load in loads[1]:
        load.wait()
    norms = lax.fori_loop(3, 5, step, norms)
    pl.semaphore_wait(barrier, n_row - 1 + n_chip)
    q_load.wait()
    halo_start(0, HALO_EARLY)
    scatter_start(0)
    scatter_start(1)
    for load in loads[2]:
        load.wait()
    norms = lax.fori_loop(5, 8, step, norms)
    scatter_start(2)
    norms = group(8 * GROUP, channels - 8 * GROUP, norms)
    part[:, NORM_AT : NORM_AT + 128] = interleave(norms).astype(part.dtype)
    scatter_start(3)

    @pl.when(row == 0)
    def _():
        halo_buf[0] = jnp.zeros_like(halo_buf[0])

    @pl.when(row == n_row - 1)
    def _():
        halo_buf[1] = jnp.zeros_like(halo_buf[1])

    gate_load.wait()
    frames, rows, width = q_buf.shape[:3]
    for f in range(frames):
        for r in range(rows):
            @pl.loop(0, width // 16)
            def _(i):
                cut = pl.ds(pl.multiple_of(16 * i, 16), 16)
                gate = gate_buf[f, r, cut].astype(jnp.float32)
                silu_buf[f, r, cut] = gate / (1.0 + jnp.exp(-gate))

    sums = part[chunk(row)].astype(jnp.float32)

    def add(i, sums):
        scatter(lax.rem(row + i, n_row)).wait_recv()
        return sums + rx[i].astype(jnp.float32)

    sums = lax.fori_loop(1, n_row, add, sums)
    even, odd = sums[:8], sums[8:]
    own_total = even + odd
    total[...] = own_total
    pair = pltpu.make_async_remote_copy(
        src_ref=total,
        dst_ref=pair_rx,
        send_sem=pair_send,
        recv_sem=pair_recv,
        device_id=(partner, row),
        device_id_type=MESH,
    )
    pair.start()
    pair.wait_recv()
    other = pair_rx[...]
    chip_total[...] = (own_total + other).astype(chip_total.dtype)

    def pass_on(i):
        return pltpu.make_async_remote_copy(
            src_ref=chip_total,
            dst_ref=chip_rx.at[i],
            send_sem=chip_send.at[i],
            recv_sem=chip_recv.at[i],
            device_id=(frame + 2 * i, row),
            device_id_type=MESH,
        )

    for i in range(1, n_chip):
        @pl.when(chip + i < n_chip)
        def _():
            pass_on(i).start()

    halo_start(HALO_EARLY, HALO_MORE)
    before[...] = jnp.where(core == 1, other, jnp.zeros_like(other))
    for i in range(1, n_chip):
        @pl.when(chip >= i)
        def _():
            pass_on(i).wait_recv()
            before[...] += chip_rx[i].astype(jnp.float32)

    first = before[...] + even
    mine[...] = jnp.concatenate([first, first + odd], axis=0).astype(mine.dtype)
    own = pltpu.make_async_copy(mine, states_buf.at[chunk(row)], own_sem)
    own.start()

    def gather(i):
        return pltpu.make_async_remote_copy(
            src_ref=mine,
            dst_ref=states_buf.at[chunk(row)],
            send_sem=ag_send.at[i],
            recv_sem=ag_recv.at[i],
            device_id=(frame, lax.rem(row + i, n_row)),
            device_id_type=MESH,
        )

    @pl.loop(1, n_row)
    def _(i):
        gather(i).start()

    halo_start(HALO_MORE, whole + 1)

    @pl.loop(1, n_row)
    def _(i):
        gather(i).wait_recv()

    own.wait()
    weight_load.wait()
    half = 128
    att = ((att_00, att_01), (att_10, att_11))
    edge = lax.broadcasted_iota(jnp.int32, (8, half), 0)

    def parity(g):
        return g[1]

    def start(g, lanes):
        first = 2 * GROUP * g[0] + GROUP * g[1]
        return first if lanes < GROUP else pl.multiple_of(first, GROUP)

    def place(g, lanes):
        return GROUP * g[0] if lanes < GROUP else pl.multiple_of(GROUP * g[0], GROUP)

    def attend(g, lanes, sources):
        heads = lanes // HEAD_DIM
        first = start(g, lanes)
        cut = pl.ds(first, lanes)
        kept = pl.ds(place(g, lanes), lanes)
        spread = (
            lax.broadcasted_iota(jnp.int32, (128, lanes), 0)
            == lax.broadcasted_iota(jnp.int32, (128, lanes), 1) // HEAD_DIM + first // HEAD_DIM
        ).astype(jnp.bfloat16)
        same = (
            lax.broadcasted_iota(jnp.int32, (lanes, lanes), 0) // HEAD_DIM
            == lax.broadcasted_iota(jnp.int32, (lanes, lanes), 1) // HEAD_DIM
        )
        states = states_buf[:, cut].astype(jnp.float32)
        norms = jnp.dot(
            states_buf[:, NORM_AT : NORM_AT + 128], spread, preferred_element_type=jnp.float32
        )

        def blocks(packed, f):
            mine = jnp.concatenate(
                [packed[16 * q + 8 * f : 16 * q + 8 * f + 8] for q in range(SIDE)], axis=0
            )
            return jnp.where(same, jnp.tile(mine, (heads, 1)), 0.0).astype(jnp.bfloat16)

        def frame_part(f):
            state, norm = blocks(states, f), blocks(norms, f)
            for r, source in sources(f):
                qf = jnp.maximum(source[:, cut], 0)
                numer = jnp.dot(qf, state, preferred_element_type=jnp.float32)
                denom = jnp.dot(qf, norm, preferred_element_type=jnp.float32)
                att[parity(g)][f][r, :, kept] = numer / (denom + 1e-6)

        return frame_part

    def mix(g, lanes, which):
        first, kept = start(g, lanes), place(g, lanes)

        def frame_part(f):
            for low in range(0, lanes, half):
                wide = min(half, lanes - low)
                cut = pl.ds(first + low, wide)
                here = pl.ds(kept + low, wide)
                weights = [[weight_buf[a, b : b + 1, cut] for b in range(3)] for a in range(3)]
                for r in which:
                    three = [att[parity(g)][f][r + a, :, here] for a in range(3)]
                    mixes = []
                    for b in range(3):
                        total = three[0] * weights[0][b]
                        for a in range(1, 3):
                            total = total + three[a] * weights[a][b]
                        mixes.append(total)
                    left = pltpu.roll(mixes[0], 1, 0)
                    first_rows = jnp.where(edge[:, :wide] > 0, left[:8], 0.0)
                    left = jnp.concatenate([first_rows, left[8:]], axis=0)
                    right = pltpu.roll(mixes[2], width - 1, 0)
                    last_rows = jnp.where(edge[:, :wide] < 7, right[-8:], 0.0)
                    right = jnp.concatenate([right[:-8], last_rows], axis=0)
                    conv = mixes[1] + left + right
                    out_ref[f, r, :, cut] = (conv * silu_buf[f, r, :, cut]).astype(out_ref.dtype)

        return frame_part

    own_rows = lambda f: [(r + 1, q_buf.at[f, r]) for r in range(rows)]
    halo_rows = lambda f: [(0, halo_buf.at[0, f]), (rows + 1, halo_buf.at[1, f])]

    def arrived(g, lanes):
        @pl.when(row > 0)
        def _():
            halo(0, g, lanes).wait_recv()

        @pl.when(row < n_row - 1)
        def _():
            halo(1, g, lanes).wait_recv()

    def run(groups, sources, which):
        attends = [attend(g, lanes, sources) for g, lanes in groups]
        mixes = [mix(g, lanes, which) for g, lanes in groups]
        steps = [(i, f) for i in range(len(groups)) for f in range(frames)]
        for at, (i, f) in enumerate(steps):
            attends[i](f)
            if at > 0:
                mixes[steps[at - 1][0]](steps[at - 1][1])
        mixes[steps[-1][0]](steps[-1][1])

    def pair_of(j):
        return [((j, 0), GROUP), ((j, 1), GROUP)]

    inner_rows, outer_rows = range(1, rows - 1), (0, rows - 1)

    @pl.loop(0, whole // 2)
    def _(j):
        run(pair_of(j), own_rows, inner_rows)

    run([((whole // 2, 0), tail)], own_rows, inner_rows)

    @pl.loop(0, whole // 2)
    def _(j):
        arrived(2 * j, GROUP)
        arrived(2 * j + 1, GROUP)
        run(pair_of(j), halo_rows, outer_rows)

    arrived(whole, tail)
    run([((whole // 2, 0), tail)], halo_rows, outer_rows)

    @pl.loop(0, whole)
    def _(g):
        @pl.when(row < n_row - 1)
        def _():
            halo(0, g, GROUP).wait_send()

        @pl.when(row > 0)
        def _():
            halo(1, g, GROUP).wait_send()

    @pl.when(row < n_row - 1)
    def _():
        halo(0, whole, tail).wait_send()

    @pl.when(row > 0)
    def _():
        halo(1, whole, tail).wait_send()

    pair.wait_send()
    for i in range(1, n_chip):
        @pl.when(chip + i < n_chip)
        def _():
            pass_on(i).wait_send()

    @pl.loop(1, n_row)
    def _(i):
        scatter(lax.rem(row + i, n_row)).wait_send()
        gather(i).wait_send()


def per_device(n_frame, n_row, queries, keys, values, gate, conv_weight):
    frames, rows, width, channels = queries.shape
    tokens = rows * width
    n_chip = n_frame // 2
    groups = pl.cdiv(channels, GROUP)
    dma = pltpu.SemaphoreType.DMA
    flat = (frames, tokens, channels)
    arrays = (queries, keys.reshape(flat), values.reshape(flat), gate, conv_weight)
    return pl.pallas_call(
        lambda *refs: mixer_kernel(n_frame, n_row, *refs),
        name="mixer",
        out_shape=pltpu.VMEM(queries.shape, jnp.bfloat16),
        in_specs=[pl.BlockSpec(memory_space=pltpu.HBM)] * len(arrays),
        out_specs=pl.BlockSpec(memory_space=pltpu.VMEM),
        scratch_shapes=[
            pltpu.VMEM(flat, jnp.bfloat16),
            pltpu.VMEM(flat, jnp.bfloat16),
            pltpu.VMEM(gate.shape, jnp.bfloat16),
            pltpu.VMEM(queries.shape, jnp.bfloat16),
            pltpu.VMEM(queries.shape, jnp.float32),
            pltpu.VMEM(conv_weight.shape, jnp.float32),
            pltpu.VMEM((2, frames, width, channels), jnp.bfloat16),
            *(pltpu.VMEM((rows + 2, width, GROUP * 5), jnp.float32) for _ in range(4)),
            pltpu.VMEM((64, PACKED), jnp.bfloat16),
            pltpu.VMEM((64, PACKED), jnp.bfloat16),
            pltpu.VMEM((n_row, 16, CHUNK), jnp.bfloat16),
            pltpu.VMEM((8, CHUNK), jnp.float32),
            pltpu.VMEM((8, CHUNK), jnp.float32),
            pltpu.VMEM((8, CHUNK), jnp.bfloat16),
            pltpu.VMEM((n_chip, 8, CHUNK), jnp.bfloat16),
            pltpu.VMEM((8, CHUNK), jnp.float32),
            pltpu.VMEM((16, CHUNK), jnp.bfloat16),
            dma((3, 2)),
            dma((2, groups)),
            dma((2, groups)),
            dma((n_row,)),
            dma((n_row,)),
            dma,
            dma,
            dma((n_chip,)),
            dma((n_chip,)),
            dma((n_row,)),
            dma((n_row,)),
            dma,
            dma,
            dma,
            dma,
        ],
        compiler_params=pltpu.CompilerParams(
            collective_id=0, has_side_effects=True, vmem_limit_bytes=40 << 20
        ),
    )(*(pltpu.with_memory_space_constraint(a, pltpu.HBM) for a in arrays))


def solution(mesh):
    split = P("frame", "row", None, None)
    sizes = (mesh.shape["frame"], mesh.shape["row"])
    return jax.shard_map(
        lambda *arrays: per_device(*sizes, *arrays),
        mesh=mesh,
        in_specs=(split, split, split, split, P()),
        out_specs=split,
        check_vma=False,
    )
```

```python
import jax
import jax.numpy as jnp
from jax import lax
from jax.experimental import pallas as pl
from jax.experimental.pallas import tpu as pltpu
from jax.sharding import PartitionSpec as P

HEADS = 70
HEAD_DIM = 32
MESH = pl.DeviceIdType.MESH

GROUP = 256
PACKED = 2560
NORM_AT = 2304
CHUNK = 640
HALO_EARLY = 1
HALO_MORE = 2
SIDE = 4


def mixer_kernel(
    n_frame, n_row, q_ref, k_ref, v_ref, gate_ref, weight_ref, out_ref,
    k_buf, v_buf, gate_buf, q_buf, silu_buf, weight_buf, halo_buf, att_00, att_01, att_10, att_11, states_buf, part, rx, total, pair_rx, chip_total, chip_rx, before, mine,
    load_sem, halo_send, halo_recv, rs_send, rs_recv, pair_send, pair_recv,
    chip_send, chip_recv, ag_send, ag_recv, own_sem, gate_sem, q_sem,
    weight_sem,
):
    frame = lax.axis_index("frame")
    row = lax.axis_index("row")
    core = lax.rem(frame, 2)
    chip = frame // 2
    n_chip = n_frame // 2
    partner = frame + 1 - 2 * core
    channels = k_buf.shape[-1]

    barrier = pltpu.get_barrier_semaphore()

    @pl.loop(1, n_row)
    def _(i):
        pl.semaphore_signal(
            barrier, inc=1, device_id=(frame, lax.rem(row + i, n_row)), device_id_type=MESH
        )

    @pl.loop(1, n_chip)
    def _(i):
        pl.semaphore_signal(
            barrier, inc=1, device_id=(lax.rem(frame + 2 * i, n_frame), row), device_id_type=MESH
        )

    pl.semaphore_signal(barrier, inc=1, device_id=(partner, row), device_id_type=MESH)

    stages = (0, 768, 1536, channels)
    q_load = pltpu.make_async_copy(q_ref, q_buf, q_sem)
    loads = []
    for at, (low, high) in enumerate(zip(stages, stages[1:])):
        lanes = pl.ds(low, high - low)
        loads.append(
            [
                pltpu.make_async_copy(src.at[:, :, lanes], dst.at[:, :, lanes], load_sem.at[at, i])
                for i, (src, dst) in enumerate(((k_ref, k_buf), (v_ref, v_buf)))
            ]
        )
        for load in loads[-1]:
            load.start()
        if at == 1:
            q_load.start()
    gate_load = pltpu.make_async_copy(gate_ref, gate_buf, gate_sem)
    gate_load.start()
    weight_load = pltpu.make_async_copy(weight_ref, weight_buf, weight_sem)
    weight_load.start()

    whole = channels // GROUP
    tail = channels - whole * GROUP

    def halo(side, g, lanes):
        source, target = (3, row + 1) if side == 0 else (0, row - 1)
        first = g * GROUP if lanes < GROUP else pl.multiple_of(g * GROUP, GROUP)
        cut = pl.ds(first, lanes)
        return pltpu.make_async_remote_copy(
            src_ref=q_buf.at[:, source, :, cut],
            dst_ref=halo_buf.at[side, :, :, cut],
            send_sem=halo_send.at[side, g],
            recv_sem=halo_recv.at[side, g],
            device_id=(frame, target),
            device_id_type=MESH,
        )

    def halo_start(low, high):
        def both(g, lanes):
            @pl.when(row < n_row - 1)
            def _():
                halo(0, g, lanes).start()

            @pl.when(row > 0)
            def _():
                halo(1, g, lanes).start()

        @pl.loop(low, min(high, whole))
        def _(g):
            both(g, GROUP)

        if high > whole:
            both(whole, tail)

    part[:, channels:] = jnp.zeros((64, PACKED - channels), part.dtype)

    def group(first, width, norms):
        ones = jnp.ones((k_buf.shape[1], 128), jnp.bfloat16)
        heads = width // HEAD_DIM
        lane = lax.broadcasted_iota(jnp.int32, (HEAD_DIM, width), 1) // HEAD_DIM
        slot = lax.broadcasted_iota(jnp.int32, (HEAD_DIM, 128), 1)
        first_head = first // HEAD_DIM
        compact = []
        new_norms = []
        for f in range(2):
            kf = jnp.maximum(k_buf[f, :, pl.ds(first, width)], 0)
            vf = jnp.concatenate([v_buf[f, :, pl.ds(first, width)], ones], axis=1)
            full = lax.dot_general(
                kf, vf, (((0,), (0,)), ((), ())), preferred_element_type=jnp.float32
            )
            state = jnp.zeros((HEAD_DIM, width), jnp.float32)
            norm = norms[f]
            for h in range(heads):
                rows = full[h * HEAD_DIM : (h + 1) * HEAD_DIM]
                state = jnp.where(lane == h, rows[:, :width], state)
                norm = jnp.where(slot == first_head + h, rows[:, width:], norm)
            compact.append(state)
            new_norms.append(norm)
        part[:, pl.ds(first, width)] = interleave(compact).astype(part.dtype)
        return tuple(new_norms)

    def interleave(pair):
        return jnp.concatenate(
            [pair[f][8 * q : 8 * q + 8] for q in range(SIDE) for f in range(2)], axis=0
        )

    def chunk(o):
        return (
            pl.ds(pl.multiple_of(16 * (o // SIDE), 16), 16),
            pl.ds(pl.multiple_of(CHUNK * lax.rem(o, SIDE), 128), CHUNK),
        )

    def scatter(peer):
        i = lax.rem(peer - row + n_row, n_row)
        return pltpu.make_async_remote_copy(
            src_ref=part.at[chunk(peer)],
            dst_ref=rx.at[i],
            send_sem=rs_send.at[i],
            recv_sem=rs_recv.at[i],
            device_id=(frame, peer),
            device_id_type=MESH,
        )

    def scatter_start(j):
        for i in range(SIDE):
            peer = lax.rem(row // SIDE + i + 1, SIDE) * SIDE + j
            if i < SIDE - 1:
                scatter(peer).start()
            else:
                @pl.when(peer != row)
                def _():
                    scatter(peer).start()

    norms = tuple(jnp.zeros((HEAD_DIM, 128), jnp.float32) for _ in range(2))

    def step(g, norms):
        return group(pl.multiple_of(g * GROUP, GROUP), GROUP, norms)

    for load in loads[0]:
        load.wait()
    norms = lax.fori_loop(0, 3, step, norms)
    for load in loads[1]:
        load.wait()
    norms = lax.fori_loop(3, 5, step, norms)
    pl.semaphore_wait(barrier, n_row - 1 + n_chip)
    q_load.wait()
    halo_start(0, HALO_EARLY)
    scatter_start(0)
    scatter_start(1)
    for load in loads[2]:
        load.wait()
    norms = lax.fori_loop(5, 8, step, norms)
    scatter_start(2)
    norms = group(8 * GROUP, channels - 8 * GROUP, norms)
    part[:, NORM_AT : NORM_AT + 128] = interleave(norms).astype(part.dtype)
    scatter_start(3)

    @pl.when(row == 0)
    def _():
        halo_buf[0] = jnp.zeros_like(halo_buf[0])

    @pl.when(row == n_row - 1)
    def _():
        halo_buf[1] = jnp.zeros_like(halo_buf[1])

    gate_load.wait()
    frames, rows, width = q_buf.shape[:3]
    for f in range(frames):
        for r in range(rows):
            @pl.loop(0, width // 16)
            def _(i):
                cut = pl.ds(pl.multiple_of(16 * i, 16), 16)
                gate = gate_buf[f, r, cut].astype(jnp.float32)
                silu_buf[f, r, cut] = gate / (1.0 + jnp.exp(-gate))

    sums = part[chunk(row)].astype(jnp.float32)

    def add(i, sums):
        scatter(lax.rem(row + i, n_row)).wait_recv()
        return sums + rx[i].astype(jnp.float32)

    sums = lax.fori_loop(1, n_row, add, sums)
    even, odd = sums[:8], sums[8:]
    own_total = even + odd
    total[...] = own_total
    pair = pltpu.make_async_remote_copy(
        src_ref=total,
        dst_ref=pair_rx,
        send_sem=pair_send,
        recv_sem=pair_recv,
        device_id=(partner, row),
        device_id_type=MESH,
    )
    pair.start()
    pair.wait_recv()
    other = pair_rx[...]
    chip_total[...] = (own_total + other).astype(chip_total.dtype)

    def pass_on(i):
        return pltpu.make_async_remote_copy(
            src_ref=chip_total,
            dst_ref=chip_rx.at[i],
            send_sem=chip_send.at[i],
            recv_sem=chip_recv.at[i],
            device_id=(frame + 2 * i, row),
            device_id_type=MESH,
        )

    for i in range(1, n_chip):
        @pl.when(chip + i < n_chip)
        def _():
            pass_on(i).start()

    halo_start(HALO_EARLY, HALO_MORE)
    before[...] = jnp.where(core == 1, other, jnp.zeros_like(other))
    for i in range(1, n_chip):
        @pl.when(chip >= i)
        def _():
            pass_on(i).wait_recv()
            before[...] += chip_rx[i].astype(jnp.float32)

    first = before[...] + even
    mine[...] = jnp.concatenate([first, first + odd], axis=0).astype(mine.dtype)
    own = pltpu.make_async_copy(mine, states_buf.at[chunk(row)], own_sem)
    own.start()

    def gather(i):
        return pltpu.make_async_remote_copy(
            src_ref=mine,
            dst_ref=states_buf.at[chunk(row)],
            send_sem=ag_send.at[i],
            recv_sem=ag_recv.at[i],
            device_id=(frame, lax.rem(row + i, n_row)),
            device_id_type=MESH,
        )

    steps = [(dx, dy) for dx in range(SIDE) for dy in range(SIDE) if dx or dy]
    for dx, dy in sorted(steps, key=lambda d: ((0, 1, 3, 2)[d[0]], (0, 1, 3, 2)[d[1]])):
        peer = lax.rem(row // SIDE + dx, SIDE) * SIDE + lax.rem(row + dy, SIDE)
        gather(lax.rem(peer - row + n_row, n_row)).start()

    halo_start(HALO_MORE, whole + 1)

    @pl.loop(1, n_row)
    def _(i):
        gather(i).wait_recv()

    own.wait()
    weight_load.wait()
    half = 128
    att = ((att_00, att_01), (att_10, att_11))
    edge = lax.broadcasted_iota(jnp.int32, (8, half), 0)

    def parity(g):
        return g[1]

    def start(g, lanes):
        first = 2 * GROUP * g[0] + GROUP * g[1]
        return first if lanes < GROUP else pl.multiple_of(first, GROUP)

    def place(g, lanes):
        return GROUP * g[0] if lanes < GROUP else pl.multiple_of(GROUP * g[0], GROUP)

    def attend(g, lanes, sources):
        heads = lanes // HEAD_DIM
        first = start(g, lanes)
        cut = pl.ds(first, lanes)
        kept = pl.ds(place(g, lanes), lanes)
        spread = (
            lax.broadcasted_iota(jnp.int32, (128, lanes), 0)
            == lax.broadcasted_iota(jnp.int32, (128, lanes), 1) // HEAD_DIM + first // HEAD_DIM
        ).astype(jnp.bfloat16)
        same = (
            lax.broadcasted_iota(jnp.int32, (lanes, lanes), 0) // HEAD_DIM
            == lax.broadcasted_iota(jnp.int32, (lanes, lanes), 1) // HEAD_DIM
        )
        states = states_buf[:, cut].astype(jnp.float32)
        norms = jnp.dot(
            states_buf[:, NORM_AT : NORM_AT + 128], spread, preferred_element_type=jnp.float32
        )

        def blocks(packed, f):
            mine = jnp.concatenate(
                [packed[16 * q + 8 * f : 16 * q + 8 * f + 8] for q in range(SIDE)], axis=0
            )
            return jnp.where(same, jnp.tile(mine, (heads, 1)), 0.0).astype(jnp.bfloat16)

        def frame_part(f):
            state, norm = blocks(states, f), blocks(norms, f)
            for r, source in sources(f):
                qf = jnp.maximum(source[:, cut], 0)
                numer = jnp.dot(qf, state, preferred_element_type=jnp.float32)
                denom = jnp.dot(qf, norm, preferred_element_type=jnp.float32)
                att[parity(g)][f][r, :, kept] = numer / (denom + 1e-6)

        return frame_part

    def mix(g, lanes, which):
        first, kept = start(g, lanes), place(g, lanes)

        def frame_part(f):
            for low in range(0, lanes, half):
                wide = min(half, lanes - low)
                cut = pl.ds(first + low, wide)
                here = pl.ds(kept + low, wide)
                weights = [[weight_buf[a, b : b + 1, cut] for b in range(3)] for a in range(3)]
                for r in which:
                    three = [att[parity(g)][f][r + a, :, here] for a in range(3)]
                    mixes = []
                    for b in range(3):
                        total = three[0] * weights[0][b]
                        for a in range(1, 3):
                            total = total + three[a] * weights[a][b]
                        mixes.append(total)
                    left = pltpu.roll(mixes[0], 1, 0)
                    first_rows = jnp.where(edge[:, :wide] > 0, left[:8], 0.0)
                    left = jnp.concatenate([first_rows, left[8:]], axis=0)
                    right = pltpu.roll(mixes[2], width - 1, 0)
                    last_rows = jnp.where(edge[:, :wide] < 7, right[-8:], 0.0)
                    right = jnp.concatenate([right[:-8], last_rows], axis=0)
                    conv = mixes[1] + left + right
                    out_ref[f, r, :, cut] = (conv * silu_buf[f, r, :, cut]).astype(out_ref.dtype)

        return frame_part

    own_rows = lambda f: [(r + 1, q_buf.at[f, r]) for r in range(rows)]
    halo_rows = lambda f: [(0, halo_buf.at[0, f]), (rows + 1, halo_buf.at[1, f])]

    def arrived(g, lanes):
        @pl.when(row > 0)
        def _():
            halo(0, g, lanes).wait_recv()

        @pl.when(row < n_row - 1)
        def _():
            halo(1, g, lanes).wait_recv()

    def run(groups, sources, which):
        attends = [attend(g, lanes, sources) for g, lanes in groups]
        mixes = [mix(g, lanes, which) for g, lanes in groups]
        steps = [(i, f) for i in range(len(groups)) for f in range(frames)]
        for at, (i, f) in enumerate(steps):
            attends[i](f)
            if at > 0:
                mixes[steps[at - 1][0]](steps[at - 1][1])
        mixes[steps[-1][0]](steps[-1][1])

    def pair_of(j):
        return [((j, 0), GROUP), ((j, 1), GROUP)]

    inner_rows, outer_rows = range(1, rows - 1), (0, rows - 1)

    @pl.loop(0, whole // 2)
    def _(j):
        run(pair_of(j), own_rows, inner_rows)

    run([((whole // 2, 0), tail)], own_rows, inner_rows)

    @pl.loop(0, whole // 2)
    def _(j):
        arrived(2 * j, GROUP)
        arrived(2 * j + 1, GROUP)
        run(pair_of(j), halo_rows, outer_rows)

    arrived(whole, tail)
    run([((whole // 2, 0), tail)], halo_rows, outer_rows)

    @pl.loop(0, whole)
    def _(g):
        @pl.when(row < n_row - 1)
        def _():
            halo(0, g, GROUP).wait_send()

        @pl.when(row > 0)
        def _():
            halo(1, g, GROUP).wait_send()

    @pl.when(row < n_row - 1)
    def _():
        halo(0, whole, tail).wait_send()

    @pl.when(row > 0)
    def _():
        halo(1, whole, tail).wait_send()

    pair.wait_send()
    for i in range(1, n_chip):
        @pl.when(chip + i < n_chip)
        def _():
            pass_on(i).wait_send()

    @pl.loop(1, n_row)
    def _(i):
        scatter(lax.rem(row + i, n_row)).wait_send()
        gather(i).wait_send()


def per_device(n_frame, n_row, queries, keys, values, gate, conv_weight):
    frames, rows, width, channels = queries.shape
    tokens = rows * width
    n_chip = n_frame // 2
    groups = pl.cdiv(channels, GROUP)
    dma = pltpu.SemaphoreType.DMA
    flat = (frames, tokens, channels)
    arrays = (queries, keys.reshape(flat), values.reshape(flat), gate, conv_weight)
    return pl.pallas_call(
        lambda *refs: mixer_kernel(n_frame, n_row, *refs),
        name="mixer",
        out_shape=pltpu.VMEM(queries.shape, jnp.bfloat16),
        in_specs=[pl.BlockSpec(memory_space=pltpu.HBM)] * len(arrays),
        out_specs=pl.BlockSpec(memory_space=pltpu.VMEM),
        scratch_shapes=[
            pltpu.VMEM(flat, jnp.bfloat16),
            pltpu.VMEM(flat, jnp.bfloat16),
            pltpu.VMEM(gate.shape, jnp.bfloat16),
            pltpu.VMEM(queries.shape, jnp.bfloat16),
            pltpu.VMEM(queries.shape, jnp.float32),
            pltpu.VMEM(conv_weight.shape, jnp.float32),
            pltpu.VMEM((2, frames, width, channels), jnp.bfloat16),
            *(pltpu.VMEM((rows + 2, width, GROUP * 5), jnp.float32) for _ in range(4)),
            pltpu.VMEM((64, PACKED), jnp.bfloat16),
            pltpu.VMEM((64, PACKED), jnp.bfloat16),
            pltpu.VMEM((n_row, 16, CHUNK), jnp.bfloat16),
            pltpu.VMEM((8, CHUNK), jnp.float32),
            pltpu.VMEM((8, CHUNK), jnp.float32),
            pltpu.VMEM((8, CHUNK), jnp.bfloat16),
            pltpu.VMEM((n_chip, 8, CHUNK), jnp.bfloat16),
            pltpu.VMEM((8, CHUNK), jnp.float32),
            pltpu.VMEM((16, CHUNK), jnp.bfloat16),
            dma((3, 2)),
            dma((2, groups)),
            dma((2, groups)),
            dma((n_row,)),
            dma((n_row,)),
            dma,
            dma,
            dma((n_chip,)),
            dma((n_chip,)),
            dma((n_row,)),
            dma((n_row,)),
            dma,
            dma,
            dma,
            dma,
        ],
        compiler_params=pltpu.CompilerParams(
            collective_id=0, has_side_effects=True, vmem_limit_bytes=40 << 20
        ),
    )(*(pltpu.with_memory_space_constraint(a, pltpu.HBM) for a in arrays))


def solution(mesh):
    split = P("frame", "row", None, None)
    sizes = (mesh.shape["frame"], mesh.shape["row"])
    return jax.shard_map(
        lambda *arrays: per_device(*sizes, *arrays),
        mesh=mesh,
        in_specs=(split, split, split, split, P()),
        out_specs=split,
        check_vma=False,
    )
```
